512 devices in a mesh: pipe: 8 (over y_hi, core), ctx: 16 (over z, y_lo), dp: 4 (over x).
Axes of the slice: x: 4, y: 8 (y_hi: 4, y_lo: 2; y = y_hi * 2 + y_lo), z: 8, core: 2. Of those that a mesh axis runs over, the one named last changes fastest.
Arguments:
- state: bfloat16 [8, 4, 2048, 1024], P('pipe', 'dp', 'ctx'), may hold values from -36 to 36
- weights: bfloat16 [2, 8, 1024, 256], P(None, 'pipe'), may hold values from -0.1875 to 0.1875
- out_grad: bfloat16 [2, 8, 4, 2048, 1024], P(None, 'pipe', 'dp', 'ctx'), may hold values from -0.59765625 to 0.59765625
- start_span: int32 [8, 4], P(None, 'dp'), may hold values from 0 to 1
- block_order: int32 [32], replicated, may hold values from 0 to 31, each once
Outputs:
- state_out: bfloat16 [8, 4, 2048, 1024], P('pipe', 'dp', 'ctx')
- weight_grads: float32 [2, 8, 1024, 256], P(None, 'pipe')
The draws below stay inside these ranges and needn't reach their ends.
All inputs are finite; a program needn't handle non-finite values.
Results may differ from the reference program's by a relative error of at most 0.012.
Values may be sent and summed in bfloat16 or wider, within the bound.
No kernel may reach another device: no remote copies, remote signals or barrier semaphores. Data moves between devices by JAX's collectives and lax.ppermute only.
A program may use at most 64 MiB of HBM per device.

```python
import math
import jax
import jax.numpy as jnp
from jax import lax

HQ = 8
HD = 128
G = 1024
S_DEV = 128
TICKS = 2
SPANS = 2
SECTIONS = 8
MB = 4
SEQ = 2048
HALVES = 32
N_CTX = 16


def draw_state(key, part):
    key_list = jax.random.split(key, 3)
    shape = (SECTIONS, MB, SEQ, G)
    base_values = jnp.clip(jax.random.normal(key_list[0], shape, jnp.float32), -4.0, 4.0)
    row_scales = jnp.exp(jax.random.uniform(key_list[1], (SECTIONS, MB, SEQ, 1), jnp.float32, math.log(0.3), math.log(3.0)))
    column_scales = jnp.exp(jax.random.uniform(key_list[2], (1, 1, 1, G), jnp.float32, math.log(0.3), math.log(3.0)))
    return (base_values * row_scales * column_scales).astype(jnp.bfloat16)


def place_ends(result, rng, least, largest):
    longest = result.shape.index(max(result.shape))
    spots = []
    for shift in (0, 1):
        where = [jax.random.randint(jax.random.fold_in(rng, axis), (), 0, length) for axis, length in enumerate(result.shape)]
        where[longest] = (where[longest] + shift) % result.shape[longest]
        spots.append(tuple(where))
    return result.at[spots[0]].set(least).at[spots[1]].set(largest)


def block_levels(stream_key, shape, cuts, least, largest):
    level, own = 1.0, jax.random.fold_in(stream_key, 6)
    for dim, parts in cuts:
        draws = jnp.exp(jax.random.uniform(jax.random.fold_in(own, dim), (parts,), jnp.float32, least / len(cuts), largest / len(cuts)))
        level = level * jnp.repeat(draws, shape[dim] // parts).reshape([-1 if axis == dim else 1 for axis in range(len(shape))])
    return level


def centred(own_key, shape, deviation, limit, cuts=(), kind=jnp.bfloat16):
    factor_of = block_levels(own_key, shape, cuts, -0.22, 0.18) if cuts else 1.0
    entries = jax.random.normal(own_key, shape, jnp.float32) * deviation * factor_of
    return jnp.minimum(jnp.maximum(entries, -limit), limit).astype(kind)


def setup_inputs(seed: int = 0) -> dict:
    arg_keys = jax.random.split(jax.random.key(seed), 6)
    state = draw_state(jax.random.fold_in(arg_keys[5], 71), 0)
    weights = centred(arg_keys[1], (SPANS, SECTIONS, G, 2 * HD), G ** -0.5, 0.1875, ((1, 8),))
    out_grad = centred(arg_keys[2], (TICKS, SECTIONS, MB, SEQ, G), 0.1, 0.59765625, ((1, 8), (2, 4), (3, 16)))
    start_span = place_ends(jax.random.randint(arg_keys[3], (SECTIONS, MB), 0, 2), jax.random.fold_in(arg_keys[3], 1), 0, 1).astype(jnp.int32)
    block_order = jax.random.permutation(arg_keys[4], HALVES).astype(jnp.int32)
    return {"state": state, "weights": weights, "out_grad": out_grad, "start_span": start_span, "block_order": block_order}


EPS = 1e-05

def rms_scale(values):
    return lax.rsqrt(lax.optimization_barrier(jnp.mean(values * values, axis=-1, keepdims=True)) + EPS)

def apply_layer(carried, weight, upstream, positions):
    widened = carried.astype(jnp.float32)
    normed = (widened * rms_scale(widened)).astype(jnp.bfloat16)
    split_heads = widened.reshape(SEQ, HQ, HD)
    queries = (split_heads * rms_scale(split_heads)).astype(jnp.bfloat16)
    projected = jnp.dot(normed, weight, preferred_element_type=jnp.float32)
    key_raw = projected[:, :HD]
    key_scale = rms_scale(key_raw)
    key_unit = key_raw * key_scale
    packed = jnp.concatenate([key_unit, projected[:, HD:]], axis=1).astype(jnp.bfloat16)
    key_rows = packed[:, :HD].astype(jnp.float32)
    value_rows = packed[:, HD:].astype(jnp.float32)
    query_wide = queries.astype(jnp.float32)
    grad_wide = upstream.reshape(SEQ, HQ, HD).astype(jnp.float32)
    score_scale = 1.0 / math.sqrt(HD)

    def query_block(block_index):
        first_row = block_index * S_DEV
        query_part = lax.dynamic_slice_in_dim(query_wide, first_row, S_DEV, 0)
        grad_part = lax.dynamic_slice_in_dim(grad_wide, first_row, S_DEV, 0)
        own_positions = lax.dynamic_slice_in_dim(positions, first_row, S_DEV, 0)
        causal = positions[None, :] <= own_positions[:, None]
        scores = jnp.einsum('qhd,kd->hqk', query_part, key_rows) * score_scale
        exponent = jnp.where(causal[None], jnp.exp(scores), 0.0)
        total_weight = lax.optimization_barrier(jnp.sum(exponent, axis=-1, keepdims=True))
        probs = lax.optimization_barrier((exponent / total_weight).astype(jnp.bfloat16)).astype(jnp.float32)
        attended = jnp.einsum('hqk,kd->qhd', probs, value_rows)
        row_delta = jnp.einsum('qhd,qhd->hq', grad_part, attended)
        value_grad = jnp.einsum('hqk,qhd->kd', probs, grad_part)
        prob_grad = jnp.einsum('qhd,kd->hqk', grad_part, value_rows)
        score_grad = lax.optimization_barrier((probs * (prob_grad - row_delta[..., None]) * score_scale).astype(jnp.bfloat16)).astype(jnp.float32)
        key_grad = jnp.einsum('hqk,qhd->kd', score_grad, query_part)
        term = lax.optimization_barrier(jnp.concatenate([key_grad, value_grad], axis=1).astype(jnp.bfloat16)).astype(jnp.float32)
        return (attended, term)
    attended, terms = lax.map(query_block, jnp.arange(N_CTX, dtype=jnp.int32))
    output = attended.reshape(SEQ, HQ * HD)
    updated = (widened + output * rms_scale(output)).astype(jnp.bfloat16)
    key_sums = lax.optimization_barrier(jnp.sum(terms, axis=0))
    key_delta = key_sums[:, :HD]
    key_back = key_scale * (key_delta - key_unit * lax.optimization_barrier(jnp.mean(key_delta * key_unit, axis=-1, keepdims=True)))
    grad_rows = jnp.concatenate([key_back, key_sums[:, HD:]], axis=1).astype(jnp.bfloat16)
    return (updated, jnp.dot(normed.T, grad_rows, preferred_element_type=jnp.float32))

def reference(state, weights, out_grad, start_span, block_order):
    half_len = SEQ // HALVES
    row_ids = jnp.arange(SEQ, dtype=jnp.int32)
    positions = (block_order[row_ids // half_len] * half_len + row_ids % half_len).astype(jnp.int32)
    spans = start_span
    carried = state.reshape(SECTIONS * MB, SEQ, G)
    weight_grads = jnp.zeros((SPANS, SECTIONS, G, 2 * HD), jnp.float32)
    section_ids = jnp.arange(SECTIONS, dtype=jnp.int32)
    for tick_index in range(TICKS):
        weight_items = weights[spans, section_ids[:, None]].reshape(SECTIONS * MB, G, 2 * HD)
        upstream = out_grad[tick_index].reshape(SECTIONS * MB, SEQ, G)
        updated, item_grads = lax.map(lambda triple: apply_layer(triple[0], triple[1], triple[2], positions), (carried, weight_items, upstream))
        item_grads = item_grads.reshape(SECTIONS, MB, G, 2 * HD)
        span_mask = (jnp.arange(SPANS, dtype=jnp.int32)[:, None, None] == spans[None, :, :]).astype(jnp.float32)
        weight_grads = weight_grads + lax.optimization_barrier(jnp.sum(span_mask[:, :, :, None, None] * item_grads[None], axis=2))
        updated = updated.reshape(SECTIONS, MB, SEQ, G)
        carried = jnp.roll(updated, 1, axis=0).reshape(SECTIONS * MB, SEQ, G)
        spans = jnp.concatenate([1 - spans[-1:], spans[:-1]], axis=0)
    return (carried.reshape(SECTIONS, MB, SEQ, G), weight_grads)
```

```python
import math

import jax
import jax.numpy as jnp
from jax import lax
from jax.sharding import PartitionSpec as P

EPS = 1e-05


def from_behind(block, axis, distance):
    devices = range(lax.axis_size(axis))
    route = [((i - distance) % len(devices), i) for i in devices]
    return lax.ppermute(block, axis, route)


def rms_scale(values):
    return lax.rsqrt(jnp.mean(values * values, axis=-1, keepdims=True) + EPS)


def token_positions(block_order, seq_total):
    half_count = block_order.shape[0]
    half_len = seq_total // half_count
    row_ids = jnp.arange(seq_total, dtype=jnp.int32)
    selected = (row_ids // half_len)[:, None] == jnp.arange(half_count, dtype=jnp.int32)[None, :]
    block_ids = jnp.sum(jnp.where(selected, block_order[None, :], 0), axis=1)
    return block_ids * half_len + row_ids % half_len


def swap(blocks, axes):
    return lax.all_to_all(blocks, axes, 0, 0, tiled=True)


def repeat_rows(rows, count):
    return jnp.broadcast_to(rows[None], (count,) + rows.shape)


def project(carried, weight):
    tok_rows, feat_width = carried.shape
    head_dim = weight.shape[1] // 2
    widened = carried.astype(jnp.float32)
    normed = (widened * rms_scale(widened)).astype(jnp.bfloat16)
    split_heads = widened.reshape(tok_rows, feat_width // head_dim, head_dim)
    queries = (split_heads * rms_scale(split_heads)).astype(jnp.bfloat16)
    projected = jnp.dot(normed, weight, preferred_element_type=jnp.float32)
    key_raw = projected[:, :head_dim]
    key_scale = rms_scale(key_raw)
    key_unit = key_raw * key_scale
    own_rows = jnp.concatenate([key_unit, projected[:, head_dim:]], axis=1).astype(jnp.bfloat16)
    return widened, normed, queries, key_scale, key_unit, own_rows


def forward(widened, queries, key_rows, value_rows, causal, score_scale):
    tok_rows, feat_width = widened.shape
    scores = (
        jnp.einsum("qhd,kd->hqk", queries, key_rows, preferred_element_type=jnp.float32)
        * score_scale
    )
    exponent = jnp.where(causal[None], jnp.exp(scores), 0.0)
    total_weight = jnp.sum(exponent, axis=-1, keepdims=True)
    probs = (exponent / total_weight).astype(jnp.bfloat16)
    attended = jnp.einsum("hqk,kd->qhd", probs, value_rows, preferred_element_type=jnp.float32)
    output = attended.reshape(tok_rows, feat_width)
    updated = (widened + output * rms_scale(output)).astype(jnp.bfloat16)
    return probs, attended, updated


def backward(probs, attended, queries, value_rows, upstream, score_scale):
    upstream = upstream.reshape(queries.shape)
    row_delta = jnp.sum(upstream.astype(jnp.float32) * attended, axis=-1).transpose(1, 0)
    value_grad = jnp.einsum("hqk,qhd->kd", probs, upstream, preferred_element_type=jnp.float32)
    prob_grad = jnp.einsum("qhd,kd->hqk", upstream, value_rows, preferred_element_type=jnp.float32)
    score_grad = (
        probs.astype(jnp.float32) * (prob_grad - row_delta[..., None]) * score_scale
    ).astype(jnp.bfloat16)
    key_grad = jnp.einsum("hqk,qhd->kd", score_grad, queries, preferred_element_type=jnp.float32)
    return jnp.concatenate([key_grad, value_grad], axis=1).astype(jnp.bfloat16)


def finish(received, normed, key_scale, key_unit):
    head_dim = key_unit.shape[1]
    key_sums = jnp.sum(received.astype(jnp.float32), axis=0)
    key_delta = key_sums[:, :head_dim]
    key_back = key_scale * (
        key_delta - key_unit * jnp.mean(key_delta * key_unit, axis=-1, keepdims=True)
    )
    grad_rows = jnp.concatenate([key_back, key_sums[:, head_dim:]], axis=1).astype(jnp.bfloat16)
    return lax.dot_general(
        normed, grad_rows, (((0,), (0,)), ((), ())), preferred_element_type=jnp.float32
    )


def shards(state, weights, out_grad, start_span, block_order):
    tok_rows = state.shape[2]
    feat_width = state.shape[3]
    head_dim = weights.shape[3] // 2
    span_count = weights.shape[0]
    section_count = lax.axis_size("pipe")
    ctx_count = lax.axis_size("ctx")
    all_count = ctx_count * lax.axis_size("dp")
    seq_total = tok_rows * ctx_count
    score_scale = 1.0 / math.sqrt(head_dim)
    all_positions = token_positions(block_order, seq_total)
    own_positions = lax.dynamic_slice_in_dim(
        all_positions, lax.axis_index("ctx") * tok_rows, tok_rows
    )
    causal = all_positions[None, :] <= own_positions[:, None]
    section_index = lax.axis_index("pipe")
    start_column = start_span[:, 0]

    def span_at(tick_index):
        anchor = (section_index - tick_index) % section_count
        first_span = jnp.sum(
            jnp.where(jnp.arange(section_count, dtype=jnp.int32) == anchor, start_column, 0)
        )
        return (first_span + (anchor + tick_index) // section_count) % 2

    tick_count = out_grad.shape[0]
    carried = state[0, 0]
    waiting = None
    weight_grads = jnp.zeros((span_count, feat_width, 2 * head_dim), jnp.float32)

    def add_grads(weight_grads, received, normed, key_scale, key_unit, span_index):
        local_grad = finish(received, normed, key_scale, key_unit)
        used = jnp.arange(span_count, dtype=jnp.int32) == span_index
        return weight_grads + jnp.where(used[:, None, None], local_grad[None], 0.0)

    for tick_index in range(tick_count):
        span_index = span_at(tick_index)
        weight = lax.dynamic_index_in_dim(weights[:, 0], span_index, 0, keepdims=False)
        widened, normed, queries, key_scale, key_unit, own_rows = project(carried, weight)
        outgoing = repeat_rows(own_rows, ctx_count)
        if waiting is None:
            gathered = swap(outgoing, "ctx")
        else:
            both = swap(jnp.concatenate([outgoing, waiting[0]], axis=1), "ctx")
            gathered = both[:, :tok_rows]
            weight_grads = add_grads(weight_grads, both[:, tok_rows:], *waiting[1])
        gathered = gathered.reshape(seq_total, 2 * head_dim)
        key_rows = gathered[:, :head_dim]
        value_rows = gathered[:, head_dim:]
        probs, attended, updated = forward(
            widened, queries, key_rows, value_rows, causal, score_scale
        )
        carried = from_behind(updated, "pipe", 1)
        terms = backward(
            probs, attended, queries, value_rows, out_grad[tick_index, 0, 0], score_scale
        )
        waiting = (
            terms.reshape(ctx_count, tok_rows, 2 * head_dim),
            (normed, key_scale, key_unit, span_index),
        )
    weight_grads = add_grads(weight_grads, swap(waiting[0], "ctx"), *waiting[1])
    part_rows = feat_width // all_count
    parts = (
        weight_grads.astype(jnp.bfloat16)
        .reshape(span_count, all_count, part_rows, 2 * head_dim)
        .transpose(1, 0, 2, 3)
    )
    everyone = ("ctx", "dp")
    summed = jnp.sum(swap(parts, everyone).astype(jnp.float32), axis=0).astype(jnp.bfloat16)
    whole = swap(repeat_rows(summed, all_count), everyone)
    weight_grads = (
        whole.transpose(1, 0, 2, 3)
        .reshape(span_count, feat_width, 2 * head_dim)
        .astype(jnp.float32)
    )
    return (carried[None, None], weight_grads[:, None])


def solution(mesh):
    return jax.shard_map(
        shards,
        mesh=mesh,
        in_specs=(
            P("pipe", "dp", "ctx", None),
            P(None, "pipe", None, None),
            P(None, "pipe", "dp", "ctx", None),
            P(None, "dp"),
            P(),
        ),
        out_specs=(P("pipe", "dp", "ctx", None), P(None, "pipe", None, None)),
        check_vma=False,
    )
```

```python
import functools
import math

import jax
import jax.numpy as jnp
from jax import lax
from jax.experimental import pallas as pl
from jax.experimental.pallas import tpu as pltpu
from jax.sharding import PartitionSpec as P

EPS = 1e-05
KEY_CHUNK = 256
NT = (((1,), (1,)), ((), ()))
TN = (((0,), (0,)), ((), ()))


def from_behind(block, axis, distance):
    devices = range(lax.axis_size(axis))
    route = [((i - distance) % len(devices), i) for i in devices]
    return lax.ppermute(block, axis, route)


def swap(blocks, axes):
    return lax.all_to_all(blocks, axes, 0, 0, tiled=True)


def rms_scale(values):
    return lax.rsqrt(jnp.mean(values * values, axis=-1, keepdims=True) + EPS)


def local_call(kernel, scalar_count, operand_count, outs):
    return pl.pallas_call(
        kernel,
        out_shape=[jax.ShapeDtypeStruct(shape, kind) for shape, kind in outs],
        in_specs=[pl.BlockSpec(memory_space=pltpu.SMEM)] * scalar_count
        + [pl.BlockSpec(memory_space=pltpu.VMEM)] * operand_count,
        out_specs=[pl.BlockSpec(memory_space=pltpu.VMEM)] * len(outs),
        compiler_params=pltpu.CompilerParams(vmem_limit_bytes=24 * 1024 * 1024),
    )


def span_at(starts, tick):
    count = starts.shape[0]
    anchor = lax.rem(lax.axis_index("pipe") + (count - tick % count), count)
    return lax.rem(starts[anchor] + lax.div(anchor + tick, count), 2)


def project_kernel(
    tick, starts, x_ref, weight_ref, *refs
):
    terms_ref = refs[0] if len(refs) == 7 else None
    kept_ref, query_ref, normed_ref, unit_ref, scale_ref, out_ref = refs[-6:]
    tok_rows, feat_width = x_ref.shape
    head_dim = unit_ref.shape[1]
    kept_ref[...] = x_ref[...]
    widened = x_ref[...].astype(jnp.float32)
    total = jnp.zeros((tok_rows, 1), jnp.float32)
    for head in range(feat_width // head_dim):
        part = widened[:, head * head_dim : (head + 1) * head_dim]
        square_sum = jnp.sum(part * part, axis=-1, keepdims=True)
        total = total + square_sum
        query = part * lax.rsqrt(square_sum * (1.0 / head_dim) + EPS)
        query_ref[head * tok_rows : (head + 1) * tok_rows, :] = query.astype(jnp.bfloat16)
    normed = (widened * lax.rsqrt(total * (1.0 / feat_width) + EPS)).astype(jnp.bfloat16)
    normed_ref[...] = normed
    projected = jnp.dot(normed, weight_ref[span_at(starts, tick)], preferred_element_type=jnp.float32)
    key_raw = projected[:, :head_dim]
    key_scale = rms_scale(key_raw)
    key_unit = key_raw * key_scale
    unit_ref[...] = key_unit
    scale_ref[...] = key_scale
    keys = key_unit.astype(jnp.bfloat16)
    values = projected[:, head_dim:].astype(jnp.bfloat16)
    for index in range(out_ref.shape[0]):
        out_ref[index, :tok_rows, :head_dim] = keys
        out_ref[index, :tok_rows, head_dim:] = values
        if terms_ref is not None:
            out_ref[index, tok_rows:, :] = terms_ref[index]


def forward_kernel(order, x_ref, query_ref, rows_ref, updated_ref, exp_ref, att_ref, recip_ref):
    tok_rows, feat_width = x_ref.shape
    ctx_count, _, pair_dim = rows_ref.shape
    head_dim = pair_dim // 2
    head_count = feat_width // head_dim
    half_len = tok_rows * ctx_count // order.shape[0]
    halves = tok_rows // half_len
    queries = query_ref[...]
    factor = math.log2(math.e) / math.sqrt(head_dim)

    def positions(block, shape, axis):
        row = lax.broadcasted_iota(jnp.int32, shape, axis)
        result = order[block * halves] * half_len + row
        for half in range(1, halves):
            later = (order[block * halves + half] - half) * half_len + row
            result = jnp.where(row >= half * half_len, later, result)
        return result

    own = positions(lax.axis_index("ctx"), (1, tok_rows), 1)
    own = jnp.concatenate([own] * head_count, axis=1)
    sums = jnp.zeros((1, head_count * tok_rows), jnp.float32)
    total = jnp.zeros((head_dim, head_count * tok_rows), jnp.float32)
    blocks = KEY_CHUNK // tok_rows
    for chunk in range(ctx_count // blocks):
        first = chunk * blocks
        rows = rows_ref[first : first + blocks, :, :].reshape(KEY_CHUNK, pair_dim)
        scores = lax.dot_general(
            rows[:, :head_dim], queries, NT, preferred_element_type=jnp.float32
        )
        where = jnp.concatenate(
            [positions(first + block, (tok_rows, 1), 0) for block in range(blocks)], axis=0
        )
        exponent = jnp.where(where <= own, jnp.exp2(scores * factor), 0.0)
        sums = sums + jnp.sum(exponent, axis=0, keepdims=True)
        kept = exponent.astype(jnp.bfloat16)
        exp_ref[first * tok_rows : (first + blocks) * tok_rows, :] = kept
        total = total + lax.dot_general(
            rows[:, head_dim:], kept, TN, preferred_element_type=jnp.float32
        )
    recip = 1.0 / sums
    recip_ref[...] = recip
    attended = total * recip
    att_ref[...] = attended
    parts = [
        attended[:, head * tok_rows : (head + 1) * tok_rows].T for head in range(head_count)
    ]
    output = jnp.concatenate(parts, axis=1)
    updated_ref[...] = (x_ref[...].astype(jnp.float32) + output * rms_scale(output)).astype(
        jnp.bfloat16
    )


def backward_kernel(query_ref, rows_ref, exp_ref, att_ref, recip_ref, grad_ref, terms_ref):
    ctx_count, tok_rows, pair_dim = rows_ref.shape
    head_dim = pair_dim // 2
    head_count = grad_ref.shape[1] // head_dim
    queries = query_ref[...]
    grad = grad_ref[...].astype(jnp.float32)
    turned = jnp.concatenate(
        [grad[:, head * head_dim : (head + 1) * head_dim].T for head in range(head_count)], axis=1
    )
    turned = (turned * recip_ref[...]).astype(jnp.bfloat16)
    row_delta = jnp.sum(turned.astype(jnp.float32) * att_ref[...], axis=0, keepdims=True)
    score_scale = 1.0 / math.sqrt(head_dim)
    blocks = KEY_CHUNK // tok_rows
    for chunk in range(ctx_count // blocks):
        first = chunk * blocks
        rows = rows_ref[first : first + blocks, :, :].reshape(KEY_CHUNK, pair_dim)
        kept = exp_ref[first * tok_rows : (first + blocks) * tok_rows, :]
        prob_grad = jnp.dot(rows[:, head_dim:], turned, preferred_element_type=jnp.float32)
        score_grad = (kept.astype(jnp.float32) * (prob_grad - row_delta)).astype(jnp.bfloat16)
        key_grad = jnp.dot(score_grad, queries, preferred_element_type=jnp.float32) * score_scale
        value_grad = lax.dot_general(kept, turned, NT, preferred_element_type=jnp.float32)
        both = jnp.concatenate([key_grad, value_grad], axis=1).astype(jnp.bfloat16)
        terms_ref[first : first + blocks, :, :] = both.reshape(blocks, tok_rows, pair_dim)


def finish_kernel(starts, *refs):
    parts_ref = refs[-1]
    dp_count, ctx_count, span_count, part_rows, pair_dim = parts_ref.shape
    head_dim = pair_dim // 2
    results = []
    for tick in range((len(refs) - 1) // 4):
        received_ref, normed_ref, unit_ref, scale_ref = refs[4 * tick : 4 * tick + 4]
        tok_rows = unit_ref.shape[0]
        sums = jnp.zeros((tok_rows, pair_dim), jnp.float32)
        for index in range(received_ref.shape[0]):
            sums = sums + received_ref[index].astype(jnp.float32)
        key_delta = sums[:, :head_dim]
        key_unit = unit_ref[...]
        key_back = scale_ref[...] * (
            key_delta - key_unit * jnp.mean(key_delta * key_unit, axis=-1, keepdims=True)
        )
        grad_rows = jnp.concatenate([key_back, sums[:, head_dim:]], axis=1).astype(jnp.bfloat16)
        results.append(
            lax.dot_general(normed_ref[...], grad_rows, TN, preferred_element_type=jnp.float32)
        )
    for span in range(span_count):
        value = jnp.zeros_like(results[0])
        for tick, result in enumerate(results):
            value = value + jnp.where(span_at(starts, tick) == span, result, 0.0)
        parts_ref[:, :, span] = value.astype(jnp.bfloat16).reshape(
            dp_count, ctx_count, part_rows, pair_dim
        )


def collect_kernel(parts_ref, out_ref):
    total = parts_ref[0].astype(jnp.float32)
    for index in range(1, parts_ref.shape[0]):
        total = total + parts_ref[index].astype(jnp.float32)
    summed = total.astype(jnp.bfloat16)
    for index in range(out_ref.shape[0]):
        out_ref[index] = summed


def collect(parts, copies):
    shape = (copies,) + parts.shape[1:]
    (result,) = local_call(collect_kernel, 0, 1, [(shape, jnp.bfloat16)])(parts)
    return result


def shards(state, weights, out_grad, start_span, block_order):
    tok_rows = state.shape[2]
    feat_width = state.shape[3]
    pair_dim = weights.shape[3]
    head_dim = pair_dim // 2
    head_count = feat_width // head_dim
    span_count = weights.shape[0]
    ctx_count = lax.axis_size("ctx")
    tick_count = out_grad.shape[0]
    starts = start_span[:, 0]
    half, wide = jnp.bfloat16, jnp.float32
    stacked = head_count * tok_rows
    seq_total = tok_rows * ctx_count
    carried = state[0, 0]
    layers = weights[:, 0]
    terms = None
    visits = []
    for tick_index in range(tick_count):
        extra = [] if terms is None else [terms]
        carried, queries, normed, key_unit, key_scale, outgoing = local_call(
            functools.partial(project_kernel, tick_index),
            1,
            2 + len(extra),
            [
                ((tok_rows, feat_width), half),
                ((stacked, head_dim), half),
                ((tok_rows, feat_width), half),
                ((tok_rows, head_dim), wide),
                ((tok_rows, 1), wide),
                ((ctx_count, tok_rows * (1 + len(extra)), pair_dim), half),
            ],
        )(starts, carried, layers, *extra)
        rows = swap(outgoing, "ctx")
        if visits:
            visits[-1][0] = rows[:, tok_rows:]
        rows = rows[:, :tok_rows]
        updated, exponents, attended, recip = local_call(
            forward_kernel,
            1,
            3,
            [
                ((tok_rows, feat_width), half),
                ((seq_total, stacked), half),
                ((head_dim, stacked), wide),
                ((1, stacked), wide),
            ],
        )(block_order, carried, queries, rows)
        carried = from_behind(updated, "pipe", 1)
        (terms,) = local_call(
            backward_kernel, 0, 6, [((ctx_count, tok_rows, pair_dim), half)]
        )(queries, rows, exponents, attended, recip, out_grad[tick_index, 0, 0])
        visits.append([None, normed, key_unit, key_scale])
    visits[-1][0] = swap(terms, "ctx")
    dp_count = lax.axis_size("dp")
    shape = (dp_count, ctx_count, span_count, feat_width // (dp_count * ctx_count), pair_dim)
    operands = [value for visit in visits for value in visit]
    (parts,) = local_call(finish_kernel, 1, len(operands), [(shape, half)])(starts, *operands)
    over_dp = collect(swap(parts, "dp"), 1)[0]
    over_ctx = swap(collect(swap(over_dp, "ctx"), ctx_count), "ctx")
    whole = swap(jnp.broadcast_to(over_ctx[None], (dp_count,) + over_ctx.shape), "dp")
    weight_grads = (
        whole.transpose(2, 0, 1, 3, 4)
        .reshape(span_count, feat_width, pair_dim)
        .astype(jnp.float32)
    )
    return (carried[None, None], weight_grads[:, None])


def solution(mesh):
    return jax.shard_map(
        shards,
        mesh=mesh,
        in_specs=(
            P("pipe", "dp", "ctx", None),
            P(None, "pipe", None, None),
            P(None, "pipe", "dp", "ctx", None),
            P(None, "dp"),
            P(),
        ),
        out_specs=(P("pipe", "dp", "ctx", None), P(None, "pipe", None, None)),
        check_vma=False,
    )
```

```python
import functools
import math

import jax
import jax.numpy as jnp
from jax import lax
from jax.experimental import pallas as pl
from jax.experimental.pallas import tpu as pltpu
from jax.sharding import PartitionSpec as P

EPS = 1e-05
KEY_CHUNK = 512
NT = (((1,), (1,)), ((), ()))
TN = (((0,), (0,)), ((), ()))


def from_behind(block, axis, distance):
    devices = range(lax.axis_size(axis))
    route = [((i - distance) % len(devices), i) for i in devices]
    return lax.ppermute(block, axis, route)


def swap(blocks, axes):
    return lax.all_to_all(blocks, axes, 0, 0, tiled=True)


def rms_scale(values):
    return lax.rsqrt(jnp.mean(values * values, axis=-1, keepdims=True) + EPS)


def local_call(kernel, scalar_count, operand_count, outs):
    return pl.pallas_call(
        kernel,
        out_shape=[jax.ShapeDtypeStruct(shape, kind) for shape, kind in outs],
        in_specs=[pl.BlockSpec(memory_space=pltpu.SMEM)] * scalar_count
        + [pl.BlockSpec(memory_space=pltpu.VMEM)] * operand_count,
        out_specs=[pl.BlockSpec(memory_space=pltpu.VMEM)] * len(outs),
        compiler_params=pltpu.CompilerParams(vmem_limit_bytes=24 * 1024 * 1024),
    )


def span_at(starts, tick):
    count = starts.shape[0]
    anchor = lax.rem(lax.axis_index("pipe") + (count - tick % count), count)
    return lax.rem(starts[anchor] + lax.div(anchor + tick, count), 2)


def project_kernel(
    tick, starts, x_ref, weight_ref, *refs
):
    terms_ref = refs[0] if len(refs) == 7 else None
    kept_ref, query_ref, normed_ref, unit_ref, scale_ref, out_ref = refs[-6:]
    tok_rows, feat_width = x_ref.shape
    head_dim = unit_ref.shape[1]
    kept_ref[...] = x_ref[...]
    widened = x_ref[...].astype(jnp.float32)
    total = jnp.zeros((tok_rows, 1), jnp.float32)
    for head in range(feat_width // head_dim):
        part = widened[:, head * head_dim : (head + 1) * head_dim]
        square_sum = jnp.sum(part * part, axis=-1, keepdims=True)
        total = total + square_sum
        query = part * lax.rsqrt(square_sum * (1.0 / head_dim) + EPS)
        query_ref[head * tok_rows : (head + 1) * tok_rows, :] = query.astype(jnp.bfloat16)
    normed = (widened * lax.rsqrt(total * (1.0 / feat_width) + EPS)).astype(jnp.bfloat16)
    normed_ref[...] = normed
    projected = jnp.dot(normed, weight_ref[span_at(starts, tick)], preferred_element_type=jnp.float32)
    key_raw = projected[:, :head_dim]
    key_scale = rms_scale(key_raw)
    key_unit = key_raw * key_scale
    unit_ref[...] = key_unit
    scale_ref[...] = key_scale
    keys = key_unit.astype(jnp.bfloat16)
    values = projected[:, head_dim:].astype(jnp.bfloat16)
    for index in range(out_ref.shape[0]):
        out_ref[index, :tok_rows, :head_dim] = keys
        out_ref[index, :tok_rows, head_dim:] = values
        if terms_ref is not None:
            out_ref[index, tok_rows:, :] = terms_ref[index]


def forward_kernel(order, x_ref, query_ref, rows_ref, updated_ref, exp_ref, att_ref, recip_ref):
    tok_rows, feat_width = x_ref.shape
    ctx_count, _, pair_dim = rows_ref.shape
    head_dim = pair_dim // 2
    head_count = feat_width // head_dim
    half_len = tok_rows * ctx_count // order.shape[0]
    halves = tok_rows // half_len
    queries = query_ref[...]
    factor = math.log2(math.e) / math.sqrt(head_dim)

    def positions(block, shape, axis):
        row = lax.broadcasted_iota(jnp.int32, shape, axis)
        result = order[block * halves] * half_len + row
        for half in range(1, halves):
            later = (order[block * halves + half] - half) * half_len + row
            result = jnp.where(row >= half * half_len, later, result)
        return result

    own = positions(lax.axis_index("ctx"), (1, tok_rows), 1)
    own = jnp.concatenate([own] * head_count, axis=1)
    sums = jnp.zeros((1, head_count * tok_rows), jnp.float32)
    total = jnp.zeros((head_dim, head_count * tok_rows), jnp.float32)
    blocks = KEY_CHUNK // tok_rows
    for chunk in range(ctx_count // blocks):
        first = chunk * blocks
        rows = rows_ref[first : first + blocks, :, :].reshape(KEY_CHUNK, pair_dim)
        scores = lax.dot_general(
            rows[:, :head_dim], queries, NT, preferred_element_type=jnp.float32
        )
        where = jnp.concatenate(
            [positions(first + block, (tok_rows, 1), 0) for block in range(blocks)], axis=0
        )
        exponent = jnp.where(where <= own, jnp.exp2(scores * factor), 0.0)
        sums = sums + jnp.sum(exponent, axis=0, keepdims=True)
        kept = exponent.astype(jnp.bfloat16)
        exp_ref[first * tok_rows : (first + blocks) * tok_rows, :] = kept
        total = total + lax.dot_general(
            rows[:, head_dim:], kept, TN, preferred_element_type=jnp.float32
        )
    recip = 1.0 / sums
    recip_ref[...] = recip
    attended = total * recip
    att_ref[...] = attended
    parts = [
        attended[:, head * tok_rows : (head + 1) * tok_rows].T for head in range(head_count)
    ]
    output = jnp.concatenate(parts, axis=1)
    updated_ref[...] = (x_ref[...].astype(jnp.float32) + output * rms_scale(output)).astype(
        jnp.bfloat16
    )


def backward_kernel(query_ref, rows_ref, exp_ref, att_ref, recip_ref, grad_ref, terms_ref):
    ctx_count, tok_rows, pair_dim = rows_ref.shape
    head_dim = pair_dim // 2
    head_count = grad_ref.shape[1] // head_dim
    queries = query_ref[...]
    grad = grad_ref[...].astype(jnp.float32)
    turned = jnp.concatenate(
        [grad[:, head * head_dim : (head + 1) * head_dim].T for head in range(head_count)], axis=1
    )
    turned = (turned * recip_ref[...]).astype(jnp.bfloat16)
    row_delta = jnp.sum(turned.astype(jnp.float32) * att_ref[...], axis=0, keepdims=True)
    score_scale = 1.0 / math.sqrt(head_dim)
    blocks = KEY_CHUNK // tok_rows
    for chunk in range(ctx_count // blocks):
        first = chunk * blocks
        rows = rows_ref[first : first + blocks, :, :].reshape(KEY_CHUNK, pair_dim)
        kept = exp_ref[first * tok_rows : (first + blocks) * tok_rows, :]
        prob_grad = jnp.dot(rows[:, head_dim:], turned, preferred_element_type=jnp.float32)
        score_grad = (kept.astype(jnp.float32) * (prob_grad - row_delta)).astype(jnp.bfloat16)
        key_grad = jnp.dot(score_grad, queries, preferred_element_type=jnp.float32) * score_scale
        value_grad = lax.dot_general(kept, turned, NT, preferred_element_type=jnp.float32)
        both = jnp.concatenate([key_grad, value_grad], axis=1).astype(jnp.bfloat16)
        terms_ref[first : first + blocks, :, :] = both.reshape(blocks, tok_rows, pair_dim)


def finish_kernel(starts, *refs):
    parts_ref = refs[-1]
    dp_count, ctx_count, span_count, part_rows, pair_dim = parts_ref.shape
    head_dim = pair_dim // 2
    results = []
    for tick in range((len(refs) - 1) // 4):
        received_ref, normed_ref, unit_ref, scale_ref = refs[4 * tick : 4 * tick + 4]
        tok_rows = unit_ref.shape[0]
        sums = jnp.zeros((tok_rows, pair_dim), jnp.float32)
        for index in range(received_ref.shape[0]):
            sums = sums + received_ref[index].astype(jnp.float32)
        key_delta = sums[:, :head_dim]
        key_unit = unit_ref[...]
        key_back = scale_ref[...] * (
            key_delta - key_unit * jnp.mean(key_delta * key_unit, axis=-1, keepdims=True)
        )
        grad_rows = jnp.concatenate([key_back, sums[:, head_dim:]], axis=1).astype(jnp.bfloat16)
        results.append(
            lax.dot_general(normed_ref[...], grad_rows, TN, preferred_element_type=jnp.float32)
        )
    for span in range(span_count):
        value = jnp.zeros_like(results[0])
        for tick, result in enumerate(results):
            value = value + jnp.where(span_at(starts, tick) == span, result, 0.0)
        parts_ref[:, :, span] = value.astype(jnp.bfloat16).reshape(
            dp_count, ctx_count, part_rows, pair_dim
        )


def collect_kernel(parts_ref, out_ref):
    total = parts_ref[0].astype(jnp.float32)
    for index in range(1, parts_ref.shape[0]):
        total = total + parts_ref[index].astype(jnp.float32)
    summed = total.astype(jnp.bfloat16)
    for index in range(out_ref.shape[0]):
        out_ref[index] = summed


def collect(parts, copies):
    shape = (copies,) + parts.shape[1:]
    (result,) = local_call(collect_kernel, 0, 1, [(shape, jnp.bfloat16)])(parts)
    return result


def shards(state, weights, out_grad, start_span, block_order):
    tok_rows = state.shape[2]
    feat_width = state.shape[3]
    pair_dim = weights.shape[3]
    head_dim = pair_dim // 2
    head_count = feat_width // head_dim
    span_count = weights.shape[0]
    ctx_count = lax.axis_size("ctx")
    tick_count = out_grad.shape[0]
    starts = start_span[:, 0]
    half, wide = jnp.bfloat16, jnp.float32
    stacked = head_count * tok_rows
    seq_total = tok_rows * ctx_count
    carried = state[0, 0]
    layers = weights[:, 0]
    terms = None
    visits = []
    for tick_index in range(tick_count):
        extra = [] if terms is None else [terms]
        carried, queries, normed, key_unit, key_scale, outgoing = local_call(
            functools.partial(project_kernel, tick_index),
            1,
            2 + len(extra),
            [
                ((tok_rows, feat_width), half),
                ((stacked, head_dim), half),
                ((tok_rows, feat_width), half),
                ((tok_rows, head_dim), wide),
                ((tok_rows, 1), wide),
                ((ctx_count, tok_rows * (1 + len(extra)), pair_dim), half),
            ],
        )(starts, carried, layers, *extra)
        rows = swap(outgoing, "ctx")
        if visits:
            visits[-1][0] = rows[:, tok_rows:]
        rows = rows[:, :tok_rows]
        updated, exponents, attended, recip = local_call(
            forward_kernel,
            1,
            3,
            [
                ((tok_rows, feat_width), half),
                ((seq_total, stacked), half),
                ((head_dim, stacked), wide),
                ((1, stacked), wide),
            ],
        )(block_order, carried, queries, rows)
        carried = from_behind(updated, "pipe", 1)
        (terms,) = local_call(
            backward_kernel, 0, 6, [((ctx_count, tok_rows, pair_dim), half)]
        )(queries, rows, exponents, attended, recip, out_grad[tick_index, 0, 0])
        visits.append([None, normed, key_unit, key_scale])
    visits[-1][0] = swap(terms, "ctx")
    dp_count = lax.axis_size("dp")
    shape = (dp_count, ctx_count, span_count, feat_width // (dp_count * ctx_count), pair_dim)
    operands = [value for visit in visits for value in visit]
    (parts,) = local_call(finish_kernel, 1, len(operands), [(shape, half)])(starts, *operands)
    over_dp = collect(swap(parts, "dp"), 1)[0]
    over_ctx = swap(collect(swap(over_dp, "ctx"), ctx_count), "ctx")
    whole = swap(jnp.broadcast_to(over_ctx[None], (dp_count,) + over_ctx.shape), "dp")
    weight_grads = (
        whole.transpose(2, 0, 1, 3, 4)
        .reshape(span_count, feat_width, pair_dim)
        .astype(jnp.float32)
    )
    return (carried[None, None], weight_grads[:, None])


def solution(mesh):
    return jax.shard_map(
        shards,
        mesh=mesh,
        in_specs=(
            P("pipe", "dp", "ctx", None),
            P(None, "pipe", None, None),
            P(None, "pipe", "dp", "ctx", None),
            P(None, "dp"),
            P(),
        ),
        out_specs=(P("pipe", "dp", "ctx", None), P(None, "pipe", None, None)),
        check_vma=False,
    )
```

```python
import functools
import math

import jax
import jax.numpy as jnp
from jax import lax
from jax.experimental import pallas as pl
from jax.experimental.pallas import tpu as pltpu
from jax.sharding import PartitionSpec as P

EPS = 1e-05
KEY_CHUNK = 512
NT = (((1,), (1,)), ((), ()))
TN = (((0,), (0,)), ((), ()))


def from_behind(block, axis, distance):
    devices = range(lax.axis_size(axis))
    route = [((i - distance) % len(devices), i) for i in devices]
    return lax.ppermute(block, axis, route)


def swap(blocks, axes):
    return lax.all_to_all(blocks, axes, 0, 0, tiled=True)


def rms_scale(values):
    return lax.rsqrt(jnp.mean(values * values, axis=-1, keepdims=True) + EPS)


def local_call(kernel, scalar_count, operand_count, outs):
    return pl.pallas_call(
        kernel,
        out_shape=[jax.ShapeDtypeStruct(shape, kind) for shape, kind in outs],
        in_specs=[pl.BlockSpec(memory_space=pltpu.SMEM)] * scalar_count
        + [pl.BlockSpec(memory_space=pltpu.VMEM)] * operand_count,
        out_specs=[pl.BlockSpec(memory_space=pltpu.VMEM)] * len(outs),
        compiler_params=pltpu.CompilerParams(vmem_limit_bytes=24 * 1024 * 1024),
    )


def span_at(starts, tick):
    count = starts.shape[0]
    anchor = lax.rem(lax.axis_index("pipe") + (count - tick % count), count)
    return lax.rem(starts[anchor] + lax.div(anchor + tick, count), 2)


def project_kernel(
    tick, starts, x_ref, weight_ref, *refs
):
    terms_ref = refs[0] if len(refs) == 7 else None
    kept_ref, query_ref, normed_ref, unit_ref, scale_ref, out_ref = refs[-6:]
    tok_rows, feat_width = x_ref.shape
    head_dim = unit_ref.shape[1]
    kept_ref[...] = x_ref[...]
    widened = x_ref[...].astype(jnp.float32)
    total = jnp.zeros((tok_rows, 1), jnp.float32)
    for head in range(feat_width // head_dim):
        part = widened[:, head * head_dim : (head + 1) * head_dim]
        square_sum = jnp.sum(part * part, axis=-1, keepdims=True)
        total = total + square_sum
        query = part * lax.rsqrt(square_sum * (1.0 / head_dim) + EPS)
        query_ref[head * tok_rows : (head + 1) * tok_rows, :] = query.astype(jnp.bfloat16)
    normed = (widened * lax.rsqrt(total * (1.0 / feat_width) + EPS)).astype(jnp.bfloat16)
    normed_ref[...] = normed
    projected = jnp.dot(normed, weight_ref[span_at(starts, tick)], preferred_element_type=jnp.float32)
    key_raw = projected[:, :head_dim]
    key_scale = rms_scale(key_raw)
    key_unit = key_raw * key_scale
    unit_ref[...] = key_unit
    scale_ref[...] = key_scale
    keys = key_unit.astype(jnp.bfloat16)
    values = projected[:, head_dim:].astype(jnp.bfloat16)
    for index in range(out_ref.shape[0]):
        out_ref[index, :tok_rows, :head_dim] = keys
        out_ref[index, :tok_rows, head_dim:] = values
        if terms_ref is not None:
            out_ref[index, tok_rows:, :] = terms_ref[index]


def forward_kernel(order, x_ref, query_ref, rows_ref, updated_ref, exp_ref, att_ref, recip_ref):
    tok_rows, feat_width = x_ref.shape
    ctx_count, _, pair_dim = rows_ref.shape
    head_dim = pair_dim // 2
    head_count = feat_width // head_dim
    half_len = tok_rows * ctx_count // order.shape[0]
    halves = tok_rows // half_len
    queries = query_ref[...]
    factor = math.log2(math.e) / math.sqrt(head_dim)

    def positions(block, shape, axis):
        row = lax.broadcasted_iota(jnp.int32, shape, axis)
        result = order[block * halves] * half_len + row
        for half in range(1, halves):
            later = (order[block * halves + half] - half) * half_len + row
            result = jnp.where(row >= half * half_len, later, result)
        return result

    own = positions(lax.axis_index("ctx"), (1, tok_rows), 1)
    own = jnp.concatenate([own] * head_count, axis=1)
    sums = jnp.zeros((1, head_count * tok_rows), jnp.float32)
    total = jnp.zeros((head_dim, head_count * tok_rows), jnp.float32)
    blocks = KEY_CHUNK // tok_rows
    for chunk in range(ctx_count // blocks):
        first = chunk * blocks
        rows = rows_ref[first : first + blocks, :, :].reshape(KEY_CHUNK, pair_dim)
        scores = lax.dot_general(
            rows[:, :head_dim], queries, NT, preferred_element_type=jnp.float32
        )
        where = jnp.concatenate(
            [positions(first + block, (tok_rows, 1), 0) for block in range(blocks)], axis=0
        )
        exponent = jnp.where(where <= own, jnp.exp2(scores * factor), 0.0)
        sums = sums + jnp.sum(exponent, axis=0, keepdims=True)
        kept = exponent.astype(jnp.bfloat16)
        exp_ref[first * tok_rows : (first + blocks) * tok_rows, :] = kept
        total = total + lax.dot_general(
            rows[:, head_dim:], kept, TN, preferred_element_type=jnp.float32
        )
    recip = 1.0 / sums
    recip_ref[...] = recip
    attended = total * recip
    att_ref[...] = attended
    parts = [
        attended[:, head * tok_rows : (head + 1) * tok_rows].T for head in range(head_count)
    ]
    output = jnp.concatenate(parts, axis=1)
    updated_ref[...] = (x_ref[...].astype(jnp.float32) + output * rms_scale(output)).astype(
        jnp.bfloat16
    )


def backward_kernel(query_ref, rows_ref, exp_ref, att_ref, recip_ref, grad_ref, terms_ref):
    ctx_count, tok_rows, pair_dim = rows_ref.shape
    head_dim = pair_dim // 2
    head_count = grad_ref.shape[1] // head_dim
    queries = query_ref[...]
    grad = grad_ref[...].astype(jnp.float32)
    turned = jnp.concatenate(
        [grad[:, head * head_dim : (head + 1) * head_dim].T for head in range(head_count)], axis=1
    )
    turned = (turned * recip_ref[...]).astype(jnp.bfloat16)
    row_delta = jnp.sum(turned.astype(jnp.float32) * att_ref[...], axis=0, keepdims=True)
    score_scale = 1.0 / math.sqrt(head_dim)
    blocks = KEY_CHUNK // tok_rows
    for chunk in range(ctx_count // blocks):
        first = chunk * blocks
        rows = rows_ref[first : first + blocks, :, :].reshape(KEY_CHUNK, pair_dim)
        kept = exp_ref[first * tok_rows : (first + blocks) * tok_rows, :]
        prob_grad = jnp.dot(rows[:, head_dim:], turned, preferred_element_type=jnp.float32)
        score_grad = (kept.astype(jnp.float32) * (prob_grad - row_delta)).astype(jnp.bfloat16)
        key_grad = jnp.dot(score_grad, queries, preferred_element_type=jnp.float32) * score_scale
        value_grad = lax.dot_general(kept, turned, NT, preferred_element_type=jnp.float32)
        both = jnp.concatenate([key_grad, value_grad], axis=1).astype(jnp.bfloat16)
        terms_ref[first : first + blocks, :, :] = both.reshape(blocks, tok_rows, pair_dim)


def finish_kernel(starts, *refs):
    parts_ref = refs[-1]
    dp_count, ctx_count, span_count, part_rows, pair_dim = parts_ref.shape
    head_dim = pair_dim // 2
    results = []
    for tick in range((len(refs) - 1) // 4):
        received_ref, normed_ref, unit_ref, scale_ref = refs[4 * tick : 4 * tick + 4]
        tok_rows = unit_ref.shape[0]
        sums = jnp.zeros((tok_rows, pair_dim), jnp.float32)
        for index in range(received_ref.shape[0]):
            sums = sums + received_ref[index].astype(jnp.float32)
        key_delta = sums[:, :head_dim]
        key_unit = unit_ref[...]
        key_back = scale_ref[...] * (
            key_delta - key_unit * jnp.mean(key_delta * key_unit, axis=-1, keepdims=True)
        )
        grad_rows = jnp.concatenate([key_back, sums[:, head_dim:]], axis=1).astype(jnp.bfloat16)
        results.append(
            lax.dot_general(normed_ref[...], grad_rows, TN, preferred_element_type=jnp.float32)
        )
    for span in range(span_count):
        value = jnp.zeros_like(results[0])
        for tick, result in enumerate(results):
            value = value + jnp.where(span_at(starts, tick) == span, result, 0.0)
        parts_ref[:, :, span] = value.astype(jnp.bfloat16).reshape(
            dp_count, ctx_count, part_rows, pair_dim
        )


def collect_kernel(parts_ref, out_ref):
    total = parts_ref[0].astype(jnp.float32)
    for index in range(1, parts_ref.shape[0]):
        total = total + parts_ref[index].astype(jnp.float32)
    summed = total.astype(jnp.bfloat16)
    for index in range(out_ref.shape[0]):
        out_ref[index] = summed


def collect(parts, copies):
    shape = (copies,) + parts.shape[1:]
    (result,) = local_call(collect_kernel, 0, 1, [(shape, jnp.bfloat16)])(parts)
    return result


def shards(state, weights, out_grad, start_span, block_order):
    tok_rows = state.shape[2]
    feat_width = state.shape[3]
    pair_dim = weights.shape[3]
    head_dim = pair_dim // 2
    head_count = feat_width // head_dim
    span_count = weights.shape[0]
    ctx_count = lax.axis_size("ctx")
    tick_count = out_grad.shape[0]
    starts = start_span[:, 0]
    half, wide = jnp.bfloat16, jnp.float32
    stacked = head_count * tok_rows
    seq_total = tok_rows * ctx_count
    carried = state[0, 0]
    layers = weights[:, 0]
    terms = None
    visits = []
    for tick_index in range(tick_count):
        extra = [] if terms is None else [terms]
        carried, queries, normed, key_unit, key_scale, outgoing = local_call(
            functools.partial(project_kernel, tick_index),
            1,
            2 + len(extra),
            [
                ((tok_rows, feat_width), half),
                ((stacked, head_dim), half),
                ((tok_rows, feat_width), half),
                ((tok_rows, head_dim), wide),
                ((tok_rows, 1), wide),
                ((ctx_count, tok_rows * (1 + len(extra)), pair_dim), half),
            ],
        )(starts, carried, layers, *extra)
        rows = swap(outgoing, "ctx")
        if visits:
            visits[-1][0] = rows[:, tok_rows:]
        rows = rows[:, :tok_rows]
        updated, exponents, attended, recip = local_call(
            forward_kernel,
            1,
            3,
            [
                ((tok_rows, feat_width), half),
                ((seq_total, stacked), half),
                ((head_dim, stacked), wide),
                ((1, stacked), wide),
            ],
        )(block_order, carried, queries, rows)
        carried = from_behind(updated, "pipe", 1)
        (terms,) = local_call(
            backward_kernel, 0, 6, [((ctx_count, tok_rows, pair_dim), half)]
        )(queries, rows, exponents, attended, recip, out_grad[tick_index, 0, 0])
        visits.append([None, normed, key_unit, key_scale])
    received, carried = lax.optimization_barrier((swap(terms, "ctx"), carried))
    visits[-1][0] = received
    dp_count = lax.axis_size("dp")
    shape = (dp_count, ctx_count, span_count, feat_width // (dp_count * ctx_count), pair_dim)
    operands = [value for visit in visits for value in visit]
    (parts,) = local_call(finish_kernel, 1, len(operands), [(shape, half)])(starts, *operands)
    over_dp = collect(swap(parts, "dp"), 1)[0]
    over_ctx = swap(collect(swap(over_dp, "ctx"), ctx_count), "ctx")
    copies = jnp.broadcast_to(over_ctx[None], (dp_count,) + over_ctx.shape)
    whole, carried = lax.optimization_barrier((swap(copies, "dp"), carried))
    weight_grads = (
        whole.transpose(2, 0, 1, 3, 4)
        .reshape(span_count, feat_width, pair_dim)
        .astype(jnp.float32)
    )
    return (carried[None, None], weight_grads[:, None])


def solution(mesh):
    return jax.shard_map(
        shards,
        mesh=mesh,
        in_specs=(
            P("pipe", "dp", "ctx", None),
            P(None, "pipe", None, None),
            P(None, "pipe", "dp", "ctx", None),
            P(None, "dp"),
            P(),
        ),
        out_specs=(P("pipe", "dp", "ctx", None), P(None, "pipe", None, None)),
        check_vma=False,
    )
```
